32 devices in a mesh: dp: 32 (over z, y, x, core).
Axes of the slice: x: 2, y: 2, z: 4, core: 2. Of those that a mesh axis runs over, the one named last changes fastest.
Arguments:
- patches: bfloat16 [24576, 1280], P('dp'), may hold values from -6 to 6
- patch_grids: int32 [192, 4, 2], P('dp'), may hold values from 0 to 16, as said below
- block_counts: int32 [32], replicated, may hold values from 0 to 6, as said below
- send_counts: int32 [5, 32], replicated, may hold values from 0 to 2, as said below
- row_table: bfloat16 [16, 1280], replicated, may hold values from -3 to 3
- col_table: bfloat16 [16, 1280], replicated, may hold values from -3 to 3
- ln_gain: bfloat16 [1280], replicated, may hold values from 0.25 to 1.75
- ln_bias: bfloat16 [1280], replicated, may hold values from -3 to 3
- w_qkv: bfloat16 [1280, 1920], replicated, may hold values from -1.2 to 1.2
- b_qkv: bfloat16 [1920], replicated, may hold values from -3 to 3
- w_out: bfloat16 [640, 1280], replicated, may hold values from -0.25 to 0.25
- b_out: bfloat16 [1280], replicated, may hold values from -3 to 3
- cotangent: bfloat16 [16384, 1280], P('dp'), may hold values from -3 to 3
Outputs:
- block_output: bfloat16 [16384, 1280], P('dp')
- grad_w_qkv: float32 [1280, 1920], P('dp')
- grad_w_out: float32 [640, 1280], P('dp')
The draws below stay inside these ranges and needn't reach their ends.
Inputs may be any that keep to these rules, and one draw needn't show every extreme that they name: `patch_grids`: in each block slot the areas h * w of its 4 images sum to at most 128; heights are 1 to 16, widths 0 to 16, width 0 meaning no image. `block_counts`: live blocks of each rank at the start; with send_counts no rank holds more than 6 live blocks during balancing, and after the last section every rank holds 2 to 4, some rank exactly 4. `send_counts`: A rank never sends more blocks than it holds live; of two partners in a section at most one sends; in every draw some rank sends exactly 2 blocks in the last section.
All inputs are finite; a program needn't handle non-finite values.
Results may differ from the reference program's by a relative error of at most 0.0075.
Values may be sent and summed in bfloat16 or wider, within the bound.
A program may use at most 128 MiB of HBM per device.

```python
import math
import jax
import jax.numpy as jnp
from jax import lax

D = 1280
HEAD = 80
HEADS = 8
BLOCK = 128
GRID = 16
IMGS = 4
BAL = 4
SLOTS = 6
MOVE = 2
SECTIONS = 5
TOKENS = 16384
DEVICES = 32


def balance_plan(key):
    base = jax.random.fold_in(key, 11)
    final_key = jax.random.fold_in(base, 1)
    chosen_key = jax.random.fold_in(base, 2)
    section_key = jax.random.fold_in(base, 3)
    all_ranks = jnp.arange(DEVICES, dtype=jnp.int32)
    counts = jax.random.randint(final_key, (DEVICES,), 2, BAL + 1).astype(jnp.int32)
    fullest = jax.random.randint(chosen_key, (), 0, DEVICES).astype(jnp.int32)
    counts = jnp.where(all_ranks == fullest, BAL, counts).astype(jnp.int32)
    sends = [None] * SECTIONS
    for section_index in reversed(range(SECTIONS)):
        bit_value = 1 << section_index
        partner = jnp.bitwise_xor(all_ranks, bit_value).astype(jnp.int32)
        lower = jnp.bitwise_and(all_ranks, bit_value) == 0
        after_own = counts
        after_other = counts[partner]
        total = after_own + after_other
        low_end = jnp.maximum(jnp.maximum(total - SLOTS, after_own - MOVE), 0)
        high_end = jnp.minimum(jnp.minimum(total, after_own + MOVE), SLOTS)
        raw_draw = jax.random.randint(jax.random.fold_in(section_key, section_index), (DEVICES,), 0, 1 << 20)
        picked = (low_end + raw_draw % (high_end - low_end + 1)).astype(jnp.int32)
        before = jnp.where(lower, picked, total - picked[partner]).astype(jnp.int32)
        if section_index == SECTIONS - 1:
            before = jnp.where(all_ranks == fullest, after_own - MOVE, before)
            before = jnp.where(partner == fullest, total - (after_other - MOVE), before).astype(jnp.int32)
        sends[section_index] = jnp.maximum(before - after_own, 0).astype(jnp.int32)
        counts = before
    return (counts, jnp.stack(sends, axis=0).astype(jnp.int32))


def draw_block_counts(key, part):
    return balance_plan(key)[0]


def draw_send_counts(key, part):
    return balance_plan(key)[1]


def draw_patch_grids(key, part):
    room_left = jnp.full((DEVICES * SLOTS,), BLOCK, jnp.int32)
    columns = []
    for image_slot in range(IMGS):
        height_draw = jax.random.randint(jax.random.fold_in(key, 2 * image_slot), (DEVICES * SLOTS,), 1, GRID + 1).astype(jnp.int32)
        width_draw = jax.random.randint(jax.random.fold_in(key, 2 * image_slot + 1), (DEVICES * SLOTS,), 1, GRID + 1).astype(jnp.int32)
        width_draw = jnp.minimum(width_draw, room_left // height_draw).astype(jnp.int32)
        room_left = (room_left - height_draw * width_draw).astype(jnp.int32)
        columns.append(jnp.stack([height_draw, width_draw], axis=-1))
    return jnp.stack(columns, axis=1).astype(jnp.int32)


def draw_w_qkv(key, part):
    inner = HEADS * HEAD
    values = jax.random.normal(key, (D, 3 * inner), jnp.float32) * (1.0 / D ** 0.5)
    return jnp.clip(values, -1.1953125, 1.1953125).astype(jnp.bfloat16)


def steps_of(key, extent, split, smallest, high):
    factor_of, own = 1.0, jax.random.fold_in(key, 6)
    for dim, blocks in split:
        steps = jnp.exp(jax.random.uniform(jax.random.fold_in(own, dim), (blocks,), jnp.float32, smallest / len(split), high / len(split)))
        factor_of = factor_of * jnp.repeat(steps, extent[dim] // blocks).reshape([-1 if axis == dim else 1 for axis in range(len(extent))])
    return factor_of


def scatter_about(own_key, dims, width, bound, shards=(), kind=jnp.bfloat16):
    values = width * jax.random.normal(own_key, dims, jnp.float32)
    if shards:
        values = values * steps_of(own_key, dims, shards, -0.22, 0.18)
    return jnp.clip(values, -bound, bound).astype(kind)


def setup_inputs(seed: int = 0) -> dict:
    key_of = jax.random.split(jax.random.key(seed), 14)
    return {
        "patches": scatter_about(key_of[0], (DEVICES * SLOTS * BLOCK, D), 1.0, 6.0, ((0, 32),)),
        "patch_grids": draw_patch_grids(jax.random.fold_in(key_of[13], 71), 0),
        "block_counts": draw_block_counts(jax.random.fold_in(key_of[13], 71), 0),
        "send_counts": draw_send_counts(jax.random.fold_in(key_of[13], 71), 0),
        "row_table": scatter_about(key_of[4], (GRID, D), 0.5, 3.0),
        "col_table": scatter_about(key_of[5], (GRID, D), 0.5, 3.0),
        "ln_gain": jnp.clip(1.0 + 0.15 * jax.random.normal(key_of[6], (D,), jnp.float32), 0.25, 1.75).astype(jnp.bfloat16),
        "ln_bias": scatter_about(key_of[7], (D,), 0.5, 3.0),
        "w_qkv": draw_w_qkv(jax.random.fold_in(key_of[13], 71), 0),
        "b_qkv": scatter_about(key_of[9], (3 * HEADS * HEAD,), 0.5, 3.0),
        "w_out": scatter_about(key_of[10], (HEADS * HEAD, D), (HEADS * HEAD) ** -0.5, 0.25),
        "b_out": scatter_about(key_of[11], (D,), 0.5, 3.0),
        "cotangent": scatter_about(key_of[12], (TOKENS, D), (24 * TOKENS ** -0.5), 3.0, ((0, 32),)),
    }


EPSILON = 1e-06

def token_layout(patch_grids):
    heights = patch_grids[:, :, 0]
    widths = patch_grids[:, :, 1]
    image_area = (heights * widths).astype(jnp.int32)
    image_end = jnp.cumsum(image_area, axis=1).astype(jnp.int32)
    image_start = (image_end - image_area).astype(jnp.int32)
    positions = jnp.arange(BLOCK, dtype=jnp.int32)[None, :, None]
    member = ((positions >= image_start[:, None, :]) & (positions < image_end[:, None, :])).astype(jnp.int32)
    image_ids = jnp.arange(patch_grids.shape[1], dtype=jnp.int32)
    in_image = lax.optimization_barrier(jnp.sum(member, axis=-1)).astype(jnp.int32)
    segment = (lax.optimization_barrier(jnp.sum(member * image_ids, axis=-1)).astype(jnp.int32) + in_image - 1).astype(jnp.int32)
    offset = (positions[:, :, 0] - lax.optimization_barrier(jnp.sum(member * image_start[:, None, :], axis=-1))).astype(jnp.int32)
    offset = offset * in_image
    span = jnp.maximum(lax.optimization_barrier(jnp.sum(member * widths[:, None, :], axis=-1)).astype(jnp.int32), 1)
    row_index = (offset // span).astype(jnp.int32)
    col_index = (offset - row_index * span).astype(jnp.int32)
    return (segment, row_index, col_index, in_image)

def embed_blocks(patch_rows, patch_grids, row_table, col_table):
    block_total = patch_grids.shape[0]
    segment, row_index, col_index, in_image = token_layout(patch_grids)
    levels = jnp.arange(row_table.shape[0], dtype=jnp.int32)
    row_hot = (row_index.reshape(-1, 1) == levels[None, :]).astype(jnp.bfloat16)
    col_hot = (col_index.reshape(-1, 1) == levels[None, :]).astype(jnp.bfloat16)
    table_sum = jnp.dot(row_hot, row_table, preferred_element_type=jnp.float32) + jnp.dot(col_hot, col_table, preferred_element_type=jnp.float32)
    embedded = (patch_rows.astype(jnp.float32) + table_sum * in_image.reshape(-1, 1).astype(jnp.float32)).astype(jnp.bfloat16)
    return (embedded.reshape(block_total, BLOCK, patch_rows.shape[1]), segment)

def layer_forward(blocks, marks, ln_gain, ln_bias, w_qkv, b_qkv, w_out, b_out):
    block_total = blocks.shape[0]
    model_width = blocks.shape[2]
    inner = w_out.shape[0]
    head_count = inner // HEAD
    rows = blocks.reshape(block_total * BLOCK, model_width).astype(jnp.float32)
    average = lax.optimization_barrier(jnp.mean(rows, axis=-1, keepdims=True))
    centred = rows - average
    variance = lax.optimization_barrier(jnp.mean(centred * centred, axis=-1, keepdims=True))
    normed = (centred * lax.rsqrt(variance + EPSILON) * ln_gain.astype(jnp.float32) + ln_bias.astype(jnp.float32)).astype(jnp.bfloat16)
    mixed = (jnp.dot(normed, w_qkv, preferred_element_type=jnp.float32) + b_qkv.astype(jnp.float32)).astype(jnp.bfloat16)
    shaped = mixed.reshape(block_total, BLOCK, 3, head_count, HEAD).astype(jnp.float32)
    query_f = shaped[:, :, 0]
    key_f = shaped[:, :, 1]
    value_f = shaped[:, :, 2]
    score_scale = 1.0 / math.sqrt(HEAD)
    scores = jnp.einsum('bqhd,bkhd->bhqk', query_f, key_f) * score_scale
    same_image = marks[:, :, None] == marks[:, None, :]
    scores = jnp.where(same_image[:, None], scores, -1e+30)
    top_score = lax.optimization_barrier(jnp.max(scores, axis=-1, keepdims=True))
    expo = jnp.exp(scores - top_score)
    probs_f = expo / lax.optimization_barrier(jnp.sum(expo, axis=-1, keepdims=True))
    probs_b = probs_f.astype(jnp.bfloat16)
    attended = jnp.einsum('bhqk,bkhd->bqhd', probs_b.astype(jnp.float32), value_f)
    attended = attended.reshape(block_total * BLOCK, inner).astype(jnp.bfloat16)
    projected = jnp.dot(attended, w_out, preferred_element_type=jnp.float32) + b_out.astype(jnp.float32)
    result = (rows + projected).astype(jnp.bfloat16)
    return (result, (normed, query_f, key_f, value_f, probs_f, probs_b, attended))

def output_backward(out_grad, saved, w_out):
    normed, query_f, key_f, value_f, probs_f, probs_b, attended = saved
    grad_out = jnp.dot(attended.T, out_grad, preferred_element_type=jnp.float32)
    attn_grad = jnp.dot(out_grad, w_out.T, preferred_element_type=jnp.float32)
    return (grad_out, attn_grad.reshape(query_f.shape))

def qkv_backward(attn_grad, saved):
    normed, query_f, key_f, value_f, probs_f, probs_b, attended = saved
    score_scale = 1.0 / math.sqrt(HEAD)
    prob_grad = jnp.einsum('bqhd,bkhd->bhqk', attn_grad, value_f)
    value_grad = jnp.einsum('bhqk,bqhd->bkhd', probs_b.astype(jnp.float32), attn_grad)
    score_grad = probs_f * (prob_grad - lax.optimization_barrier(jnp.sum(prob_grad * probs_f, axis=-1, keepdims=True))) * score_scale
    query_grad = jnp.einsum('bhqk,bkhd->bqhd', score_grad, key_f)
    key_grad = jnp.einsum('bhqk,bqhd->bkhd', score_grad, query_f)
    row_total = query_f.shape[0] * query_f.shape[1]
    mixed_grad = jnp.stack([query_grad, key_grad, value_grad], axis=2).reshape(row_total, -1).astype(jnp.bfloat16)
    return jnp.dot(normed.T, mixed_grad, preferred_element_type=jnp.float32)

def balance_anchor(block_counts, send_counts):
    all_ranks = jnp.arange(DEVICES, dtype=jnp.int32)
    slot_ids = jnp.arange(SLOTS, dtype=jnp.int32)[None, :]
    anchor = (all_ranks[:, None] * SLOTS + slot_ids).astype(jnp.int32)
    counts = block_counts.astype(jnp.int32)
    for section_index in range(SECTIONS):
        partner = jnp.bitwise_xor(all_ranks, 1 << section_index).astype(jnp.int32)
        sent_now = send_counts[section_index].astype(jnp.int32)
        received = sent_now[partner]
        their_count = counts[partner]
        staying = slot_ids < (counts - sent_now)[:, None]
        landing = (slot_ids >= counts[:, None]) & (slot_ids < (counts + received)[:, None])
        source = jnp.clip(their_count[:, None] - received[:, None] + slot_ids - counts[:, None], 0, SLOTS - 1).astype(jnp.int32)
        incoming = anchor[partner[:, None], source]
        anchor = jnp.where(staying, anchor, jnp.where(landing, incoming, 0)).astype(jnp.int32)
        counts = (counts - sent_now + received).astype(jnp.int32)
    return (anchor, counts)

def reference(patches, patch_grids, block_counts, send_counts, row_table, col_table, ln_gain, ln_bias, w_qkv, b_qkv, w_out, b_out, cotangent):
    model_width = patches.shape[1]
    embedded, segment = embed_blocks(patches, patch_grids, row_table, col_table)
    anchor, counts = balance_anchor(block_counts, send_counts)
    chosen = anchor[:, :BAL].astype(jnp.int32)
    live = jnp.arange(BAL, dtype=jnp.int32)[None, :] < counts[:, None]
    blocks = embedded[chosen]
    marks = segment[chosen].astype(jnp.float32)
    rank_grads = cotangent.reshape(DEVICES, BAL * BLOCK, model_width)

    def one_rank(carry, inputs):
        rank_blocks, rank_marks, rank_live, rank_cot = inputs
        result, saved = layer_forward(rank_blocks, rank_marks, ln_gain, ln_bias, w_qkv, b_qkv, w_out, b_out)
        token_live = (rank_live[:, None] & (rank_marks >= 0)).reshape(-1, 1)
        out_grad = jnp.where(token_live, rank_cot, jnp.zeros_like(rank_cot)).astype(jnp.bfloat16)
        grad_out, attn_grad = output_backward(out_grad, saved, w_out)
        grad_qkv = qkv_backward(attn_grad, saved)
        slot_live = jnp.repeat(rank_live, BLOCK).reshape(-1, 1)
        result = jnp.where(slot_live, result, jnp.zeros_like(result))
        return ((carry[0] + grad_qkv, carry[1] + grad_out), result)
    start = (jnp.zeros(w_qkv.shape, jnp.float32), jnp.zeros(w_out.shape, jnp.float32))
    totals, outputs = lax.scan(one_rank, start, (blocks, marks, live, rank_grads))
    return (outputs.reshape(TOKENS, model_width), totals[0], totals[1])
```

```python
import functools
import math

import jax
import jax.numpy as jnp
from jax import lax
from jax.experimental import pallas as pl
from jax.experimental.pallas import tpu as pltpu
from jax.sharding import PartitionSpec as P

HEAD = 80
BLOCK = 128
CHUNKS = 8
EPSILON = 1e-06
MESH = pl.DeviceIdType.MESH


def partner_of(me, bit):
    own = (me // (1 << bit)) % 2
    return me + (1 - 2 * own) * (1 << bit)


def greet_partners(me, bits):
    barrier = pltpu.get_barrier_semaphore()
    for bit in range(bits):
        pl.semaphore_signal(
            barrier, inc=1, device_id=(partner_of(me, bit),), device_id_type=MESH
        )
    pl.semaphore_wait(barrier, bits)


def balance_kernel(
    sections, counts_ref, sends_ref, patches_ref, marks_ref, rows_ref, tags_ref,
    slots, slot_tags, stage, stage_tags, land, land_tags, sent, landed, sent_tags, landed_tags,
):
    me = lax.axis_index("dp")
    slot_count, chunks = patches_ref.shape[0], patches_ref.shape[1]
    balanced = rows_ref.shape[0]
    spare = stage.shape[2]
    partners = [partner_of(me, q) for q in range(sections)]
    count = counts_ref[me]
    counts, leaving = [], []
    for q in range(sections):
        counts.append(count)
        leaving.append(sends_ref[q, me])
        count = count - sends_ref[q, me] + sends_ref[q, partners[q]]
    greet_partners(me, sections)

    def copies(q, k):
        made = [
            pltpu.make_async_remote_copy(
                src_ref=stage.at[q, k], dst_ref=land.at[q, k],
                send_sem=sent.at[q, k], recv_sem=landed.at[q, k],
                device_id=(partners[q],), device_id_type=MESH,
            )
        ]
        if k == 0:
            made.append(
                pltpu.make_async_remote_copy(
                    src_ref=stage_tags.at[q], dst_ref=land_tags.at[q],
                    send_sem=sent_tags.at[q], recv_sem=landed_tags.at[q],
                    device_id=(partners[q],), device_id_type=MESH,
                )
            )
        return made

    def settle(q, k, source, arrived, target, limit):
        for s in range(limit):
            fresh = arrived[0]
            for i in range(1, spare):
                fresh = jnp.where(s - counts[q] >= i, arrived[i], fresh)
            target(s, jnp.where(s < counts[q], source(s), fresh))

    def finish(q, k):
        for copy in copies(q, k):
            copy.wait_recv()
        last = q == sections - 1
        limit = balanced if last else slot_count
        blocks = patches_ref if q == 0 else slots
        out = rows_ref if last else slots

        def put(s, value):
            out[s, k] = value

        settle(q, k, lambda s: blocks[s, k], [land[q, k, i] for i in range(spare)], put, limit)
        if k == 0:
            tags = marks_ref if q == 0 else slot_tags
            out_tags = tags_ref if last else slot_tags

            def put_tags(s, value):
                out_tags[s] = value

            settle(q, k, lambda s: tags[s], [land_tags[q, i] for i in range(spare)], put_tags, limit)

    def start(q, k):
        blocks = patches_ref if q == 0 else slots
        tags = marks_ref if q == 0 else slot_tags
        for i in range(spare):
            picked = jnp.clip(counts[q] - leaving[q] + i, 0, slot_count - 1)
            stage[q, k, i] = blocks[picked, k]
            if k == 0:
                stage_tags[q, i] = tags[picked]
        for copy in copies(q, k):
            copy.start()

    for t in range(chunks + 2 * (sections - 1)):
        for q in range(sections):
            k = t - 2 * q
            if 0 <= k < chunks:
                if q > 0:
                    finish(q - 1, k)
                start(q, k)
    for k in range(chunks):
        finish(sections - 1, k)
    for q in range(sections):
        for k in range(chunks):
            for copy in copies(q, k):
                copy.wait_send()


def balance(patches, marks, block_counts, send_counts, balanced):
    slot_count = marks.shape[0]
    width = patches.shape[1]
    sections = send_counts.shape[0]
    spare = slot_count - balanced
    rows = BLOCK // CHUNKS
    vmem = pl.BlockSpec(memory_space=pltpu.VMEM)
    smem = pl.BlockSpec(memory_space=pltpu.SMEM)
    tag = marks.shape[1:]
    return pl.pallas_call(
        functools.partial(balance_kernel, sections),
        out_shape=(
            jax.ShapeDtypeStruct((balanced, CHUNKS, rows, width), patches.dtype),
            jax.ShapeDtypeStruct((balanced,) + tag, marks.dtype),
        ),
        in_specs=[smem, smem, vmem, vmem],
        out_specs=(vmem, vmem),
        scratch_shapes=[
            pltpu.VMEM((slot_count, CHUNKS, rows, width), patches.dtype),
            pltpu.VMEM((slot_count,) + tag, marks.dtype),
            pltpu.VMEM((sections, CHUNKS, spare, rows, width), patches.dtype),
            pltpu.VMEM((sections, spare) + tag, marks.dtype),
            pltpu.VMEM((sections, CHUNKS, spare, rows, width), patches.dtype),
            pltpu.VMEM((sections, spare) + tag, marks.dtype),
            pltpu.SemaphoreType.DMA((sections, CHUNKS)),
            pltpu.SemaphoreType.DMA((sections, CHUNKS)),
            pltpu.SemaphoreType.DMA((sections,)),
            pltpu.SemaphoreType.DMA((sections,)),
        ],
        compiler_params=pltpu.CompilerParams(
            collective_id=0, has_side_effects=True, vmem_limit_bytes=48 * 2**20
        ),
    )(block_counts, send_counts, patches.reshape(slot_count, CHUNKS, rows, width), marks)


def reduce_kernel(orders, *refs):
    parts = len(orders)
    levels = len(orders[0])
    ins, refs = refs[:parts], refs[parts:]
    qkv_out, last_out = refs[0], refs[1]
    scratch = refs[2:]
    kept = [scratch[p * (levels + 1)] for p in range(parts)]
    land = [scratch[p * (levels + 1) + 1:(p + 1) * (levels + 1)] for p in range(parts)]
    sent, landed = scratch[-2], scratch[-1]
    me = lax.axis_index("dp")
    side = [(me // (1 << bit)) % 2 for bit in range(levels)]
    greet_partners(me, levels)

    def bases(p):
        base, found = 0, [0]
        for s in range(1, levels):
            base = base + side[orders[p][s]] * (1 << (levels - 1 - s))
            found.append(base)
        return found

    base_of = [bases(p) for p in range(parts)]

    def copy_of(p, s):
        bit = orders[p][s]
        if s == 0:
            source = ins[p].at[:, 1 - side[0]]
        else:
            half = 1 << (levels - 1 - s)
            source = kept[p].at[
                pl.ds(base_of[p][s - 1] + (1 - side[bit]) * half, half)
            ]
        return pltpu.make_async_remote_copy(
            src_ref=source, dst_ref=land[p][s],
            send_sem=sent.at[p, s], recv_sem=landed.at[p, s],
            device_id=(partner_of(me, bit),), device_id_type=MESH,
        )

    def add(p, s):
        total = 1 << (levels - 1 - s)
        if s == 0:

            def step(j, carry):
                chip = 0
                for i in range(1, levels):
                    chip = chip + ((j // (1 << (levels - 1 - i))) % 2) * (1 << (orders[p][i] - 1))
                kept[p][j] = (
                    ins[p][chip, side[0]].astype(jnp.float32) + land[p][0][chip].astype(jnp.float32)
                ).astype(jnp.bfloat16)
                return carry

            lax.fori_loop(0, total, step, 0)
            return
        own = base_of[p][s]
        if s < levels - 1:

            def step(j, carry):
                kept[p][own + j] = (
                    kept[p][own + j].astype(jnp.float32) + land[p][s][j].astype(jnp.float32)
                ).astype(jnp.bfloat16)
                return carry

            lax.fori_loop(0, total, step, 0)
            return
        final = kept[p][own].astype(jnp.float32) + land[p][s][0].astype(jnp.float32)
        if p < parts - 1:
            width = final.shape[1]
            qkv_out[:, p * width:(p + 1) * width] = final
        else:
            last_out[...] = final

    for s in range(levels + 1):
        for p in range(parts):
            if s > 0:
                copy_of(p, s - 1).wait_recv()
                add(p, s - 1)
            if s < levels:
                copy_of(p, s).start()
    for p in range(parts):
        for s in range(levels):
            copy_of(p, s).wait_send()


def reduce_rows(parts, devices):
    levels = devices.bit_length() - 1
    bits = list(range(1, levels))
    orders = []
    for p in range(len(parts)):
        first = bits[:3]
        turn = p % len(first)
        orders.append([0] + first[turn:] + first[:turn] + bits[3:])
    shaped = [
        part.reshape(devices // 2, 2, part.shape[0] // devices, part.shape[1]) for part in parts
    ]
    vmem = pl.BlockSpec(memory_space=pltpu.VMEM)
    scratch = []
    for part in shaped:
        scratch.append(pltpu.VMEM((devices // 2,) + part.shape[2:], jnp.bfloat16))
        for s in range(levels):
            scratch.append(pltpu.VMEM((1 << (levels - 1 - s),) + part.shape[2:], jnp.bfloat16))
    count = len(parts)
    scratch += [pltpu.SemaphoreType.DMA((count, levels))] * 2
    qkv, last = shaped[0].shape, shaped[-1].shape
    return pl.pallas_call(
        functools.partial(reduce_kernel, orders),
        out_shape=(
            jax.ShapeDtypeStruct((qkv[2], (count - 1) * qkv[3]), jnp.float32),
            jax.ShapeDtypeStruct(last[2:], jnp.float32),
        ),
        in_specs=[vmem] * count,
        out_specs=(vmem, vmem),
        scratch_shapes=scratch,
        compiler_params=pltpu.CompilerParams(
            collective_id=1, has_side_effects=True, vmem_limit_bytes=56 * 2**20
        ),
    )(*shaped)


def token_layout(patch_grids):
    heights = patch_grids[:, :, 0]
    widths = patch_grids[:, :, 1]
    image_area = heights * widths
    image_end = jnp.cumsum(image_area, axis=1)
    image_start = image_end - image_area
    positions = jnp.arange(BLOCK, dtype=jnp.int32)[None, :, None]
    member = ((positions >= image_start[:, None, :]) & (positions < image_end[:, None, :])).astype(
        jnp.int32
    )
    image_ids = jnp.arange(patch_grids.shape[1], dtype=jnp.int32)
    in_image = jnp.sum(member, axis=-1)
    segment = jnp.sum(member * image_ids, axis=-1) + in_image - 1
    offset = positions[:, :, 0] - jnp.sum(member * image_start[:, None, :], axis=-1)
    offset = offset * in_image
    span = jnp.maximum(jnp.sum(member * widths[:, None, :], axis=-1), 1)
    row_index = offset // span
    col_index = offset - row_index * span
    return (segment, row_index, col_index, in_image)


def layer_forward(blocks, marks, ln_gain, ln_bias, w_qkv, b_qkv, w_out, b_out):
    block_total = blocks.shape[0]
    model_width = blocks.shape[2]
    inner = w_out.shape[0]
    head_count = inner // HEAD
    rows = blocks.reshape(block_total * BLOCK, model_width).astype(jnp.float32)
    average = jnp.mean(rows, axis=-1, keepdims=True)
    centred = rows - average
    variance = jnp.mean(centred * centred, axis=-1, keepdims=True)
    normed = (
        centred * lax.rsqrt(variance + EPSILON) * ln_gain.astype(jnp.float32)
        + ln_bias.astype(jnp.float32)
    ).astype(jnp.bfloat16)
    mixed = (
        jnp.dot(normed, w_qkv, preferred_element_type=jnp.float32) + b_qkv.astype(jnp.float32)
    ).astype(jnp.bfloat16)
    shaped = mixed.reshape(block_total, BLOCK, 3, head_count, HEAD).astype(jnp.float32)
    query_f = shaped[:, :, 0]
    key_f = shaped[:, :, 1]
    value_f = shaped[:, :, 2]
    score_scale = 1.0 / math.sqrt(HEAD)
    scores = jnp.einsum("bqhd,bkhd->bhqk", query_f, key_f) * score_scale
    same_image = marks[:, :, None] == marks[:, None, :]
    scores = jnp.where(same_image[:, None], scores, -1e30)
    top_score = jnp.max(scores, axis=-1, keepdims=True)
    expo = jnp.exp(scores - top_score)
    probs_f = expo / jnp.sum(expo, axis=-1, keepdims=True)
    probs_b = probs_f.astype(jnp.bfloat16)
    attended = jnp.einsum("bhqk,bkhd->bqhd", probs_b.astype(jnp.float32), value_f)
    attended = attended.reshape(block_total * BLOCK, inner).astype(jnp.bfloat16)
    projected = jnp.dot(attended, w_out, preferred_element_type=jnp.float32) + b_out.astype(
        jnp.float32
    )
    result = (rows + projected).astype(jnp.bfloat16)
    return (result, (normed, query_f, key_f, value_f, probs_f, probs_b, attended))


def output_backward(out_grad, saved, w_out):
    normed, query_f, key_f, value_f, probs_f, probs_b, attended = saved
    grad_out = jnp.dot(attended.T, out_grad, preferred_element_type=jnp.float32)
    attn_grad = jnp.dot(out_grad, w_out.T, preferred_element_type=jnp.float32)
    return (grad_out, attn_grad.reshape(query_f.shape))


def qkv_backward(attn_grad, saved):
    normed, query_f, key_f, value_f, probs_f, probs_b, attended = saved
    score_scale = 1.0 / math.sqrt(HEAD)
    prob_grad = jnp.einsum("bqhd,bkhd->bhqk", attn_grad, value_f)
    value_grad = jnp.einsum("bhqk,bqhd->bkhd", probs_b.astype(jnp.float32), attn_grad)
    score_grad = (
        probs_f * (prob_grad - jnp.sum(prob_grad * probs_f, axis=-1, keepdims=True)) * score_scale
    )
    query_grad = jnp.einsum("bhqk,bkhd->bqhd", score_grad, key_f)
    key_grad = jnp.einsum("bhqk,bqhd->bkhd", score_grad, query_f)
    row_total = query_f.shape[0] * query_f.shape[1]
    return [
        jnp.dot(
            normed.T,
            part.reshape(row_total, -1).astype(jnp.bfloat16),
            preferred_element_type=jnp.float32,
        ).astype(jnp.bfloat16)
        for part in (query_grad, key_grad, value_grad)
    ]


def local(
    patches,
    patch_grids,
    block_counts,
    send_counts,
    row_table,
    col_table,
    ln_gain,
    ln_bias,
    w_qkv,
    b_qkv,
    w_out,
    b_out,
    cotangent,
):
    balanced = cotangent.shape[0] // BLOCK
    width = patches.shape[1]
    devices = lax.axis_size("dp")
    own_rank = lax.axis_index("dp")
    segment, row_index, col_index, in_image = token_layout(patch_grids)
    marks = jnp.stack([segment, row_index, col_index, in_image], axis=1).astype(jnp.float32)
    marks = jnp.pad(marks, ((0, 0), (0, 8 - marks.shape[1]), (0, 0)))
    rows, tags = balance(patches, marks, block_counts, send_counts, balanced)
    live_count = block_counts[own_rank]
    for section in range(send_counts.shape[0]):
        sent_now = send_counts[section]
        live_count = live_count - sent_now[own_rank] + sent_now[own_rank ^ (1 << section)]
    rank_marks = tags[:, 0]
    levels = jnp.arange(row_table.shape[0], dtype=jnp.float32)
    here = tags[:, 3].reshape(-1, 1) > 0
    row_hot = (here & (tags[:, 1].reshape(-1, 1) == levels)).astype(jnp.bfloat16)
    col_hot = (here & (tags[:, 2].reshape(-1, 1) == levels)).astype(jnp.bfloat16)
    table_sum = jnp.dot(row_hot, row_table, preferred_element_type=jnp.float32) + jnp.dot(
        col_hot, col_table, preferred_element_type=jnp.float32
    )
    rank_blocks = (
        (rows.reshape(-1, width).astype(jnp.float32) + table_sum)
        .astype(jnp.bfloat16)
        .reshape(balanced, BLOCK, width)
    )
    rank_live = jnp.arange(balanced, dtype=jnp.int32) < live_count
    result, saved = layer_forward(
        rank_blocks, rank_marks, ln_gain, ln_bias, w_qkv, b_qkv, w_out, b_out
    )
    slot_live = jnp.repeat(rank_live, BLOCK).reshape(-1, 1)
    result = jnp.where(slot_live, result, jnp.zeros_like(result))
    token_live = (rank_live[:, None] & (rank_marks >= 0)).reshape(-1, 1)
    out_grad = jnp.where(token_live, cotangent, jnp.zeros_like(cotangent))
    grad_out, attn_grad = output_backward(out_grad, saved, w_out)
    parts = qkv_backward(attn_grad, saved) + [grad_out.astype(jnp.bfloat16)]
    qkv_rows, out_rows = reduce_rows(parts, devices)
    return (result, qkv_rows, out_rows)


def solution(mesh):
    return jax.shard_map(
        local,
        mesh=mesh,
        in_specs=(
            P("dp", None),
            P("dp", None, None),
            P(),
            P(),
            P(),
            P(),
            P(),
            P(),
            P(),
            P(),
            P(),
            P(),
            P("dp", None),
        ),
        out_specs=(P("dp", None), P("dp", None), P("dp", None)),
        check_vma=False,
    )
```

```python
import functools
import math

import jax
import jax.numpy as jnp
from jax import lax
from jax.experimental import pallas as pl
from jax.experimental.pallas import tpu as pltpu
from jax.sharding import PartitionSpec as P

HEAD = 80
BLOCK = 128
CHUNKS = 8
EPSILON = 1e-06
MESH = pl.DeviceIdType.MESH


def partner_of(me, bit):
    own = (me // (1 << bit)) % 2
    return me + (1 - 2 * own) * (1 << bit)


def greet_partners(me, bits):
    barrier = pltpu.get_barrier_semaphore()
    for bit in range(bits):
        pl.semaphore_signal(
            barrier, inc=1, device_id=(partner_of(me, bit),), device_id_type=MESH
        )
    pl.semaphore_wait(barrier, bits)


def balance_kernel(
    sections, counts_ref, sends_ref, patches_ref, marks_ref, rows_ref, tags_ref,
    slots, slot_tags, stage, stage_tags, land, land_tags, sent, landed, sent_tags, landed_tags,
):
    me = lax.axis_index("dp")
    slot_count, chunks = patches_ref.shape[0], patches_ref.shape[1]
    balanced = rows_ref.shape[0]
    spare = stage.shape[2]
    partners = [partner_of(me, q) for q in range(sections)]
    count = counts_ref[me]
    counts, leaving = [], []
    for q in range(sections):
        counts.append(count)
        leaving.append(sends_ref[q, me])
        count = count - sends_ref[q, me] + sends_ref[q, partners[q]]
    greet_partners(me, sections)

    def copies(q, k):
        made = [
            pltpu.make_async_remote_copy(
                src_ref=stage.at[q, k], dst_ref=land.at[q, k],
                send_sem=sent.at[q, k], recv_sem=landed.at[q, k],
                device_id=(partners[q],), device_id_type=MESH,
            )
        ]
        if k == 0:
            made.append(
                pltpu.make_async_remote_copy(
                    src_ref=stage_tags.at[q], dst_ref=land_tags.at[q],
                    send_sem=sent_tags.at[q], recv_sem=landed_tags.at[q],
                    device_id=(partners[q],), device_id_type=MESH,
                )
            )
        return made

    def settle(q, k, source, arrived, target, limit):
        for s in range(limit):
            fresh = arrived[0]
            for i in range(1, spare):
                fresh = jnp.where(s - counts[q] >= i, arrived[i], fresh)
            target(s, jnp.where(s < counts[q], source(s), fresh))

    def finish(q, k):
        for copy in copies(q, k):
            copy.wait_recv()
        last = q == sections - 1
        limit = balanced if last else slot_count
        blocks = patches_ref if q == 0 else slots
        out = rows_ref if last else slots

        def put(s, value):
            out[s, k] = value

        settle(q, k, lambda s: blocks[s, k], [land[q, k, i] for i in range(spare)], put, limit)
        if k == 0:
            tags = marks_ref if q == 0 else slot_tags
            out_tags = tags_ref if last else slot_tags

            def put_tags(s, value):
                if last:
                    out_tags[s, :8] = value
                    out_tags[s, 8:] = jnp.full(value.shape, jnp.where(s < count, 1.0, 0.0))
                else:
                    out_tags[s] = value

            settle(q, k, lambda s: tags[s], [land_tags[q, i] for i in range(spare)], put_tags, limit)

    def start(q, k):
        blocks = patches_ref if q == 0 else slots
        tags = marks_ref if q == 0 else slot_tags
        for i in range(spare):
            picked = jnp.clip(counts[q] - leaving[q] + i, 0, slot_count - 1)
            stage[q, k, i] = blocks[picked, k]
            if k == 0:
                stage_tags[q, i] = tags[picked]
        for copy in copies(q, k):
            copy.start()

    for t in range(chunks + 2 * (sections - 1)):
        for q in range(sections):
            k = t - 2 * q
            if 0 <= k < chunks:
                if q > 0:
                    finish(q - 1, k)
                start(q, k)
    for k in range(chunks):
        finish(sections - 1, k)
    for q in range(sections):
        for k in range(chunks):
            for copy in copies(q, k):
                copy.wait_send()


def balance(patches, marks, block_counts, send_counts, balanced):
    slot_count = marks.shape[0]
    width = patches.shape[1]
    sections = send_counts.shape[0]
    spare = slot_count - balanced
    rows = BLOCK // CHUNKS
    vmem = pl.BlockSpec(memory_space=pltpu.VMEM)
    smem = pl.BlockSpec(memory_space=pltpu.SMEM)
    tag = marks.shape[1:]
    return pl.pallas_call(
        functools.partial(balance_kernel, sections),
        out_shape=(
            jax.ShapeDtypeStruct((balanced, CHUNKS, rows, width), patches.dtype),
            jax.ShapeDtypeStruct((balanced, 2 * tag[0], tag[1]), marks.dtype),
        ),
        in_specs=[smem, smem, vmem, vmem],
        out_specs=(vmem, vmem),
        scratch_shapes=[
            pltpu.VMEM((slot_count, CHUNKS, rows, width), patches.dtype),
            pltpu.VMEM((slot_count,) + tag, marks.dtype),
            pltpu.VMEM((sections, CHUNKS, spare, rows, width), patches.dtype),
            pltpu.VMEM((sections, spare) + tag, marks.dtype),
            pltpu.VMEM((sections, CHUNKS, spare, rows, width), patches.dtype),
            pltpu.VMEM((sections, spare) + tag, marks.dtype),
            pltpu.SemaphoreType.DMA((sections, CHUNKS)),
            pltpu.SemaphoreType.DMA((sections, CHUNKS)),
            pltpu.SemaphoreType.DMA((sections,)),
            pltpu.SemaphoreType.DMA((sections,)),
        ],
        compiler_params=pltpu.CompilerParams(
            collective_id=0, has_side_effects=True, vmem_limit_bytes=48 * 2**20
        ),
    )(block_counts, send_counts, patches.reshape(slot_count, CHUNKS, rows, width), marks)


def reduce_kernel(orders, *refs):
    parts = len(orders)
    levels = len(orders[0])
    ins, refs = refs[:parts], refs[parts:]
    qkv_out, last_out = refs[0], refs[1]
    scratch = refs[2:]
    kept = [scratch[p * (levels + 1)] for p in range(parts)]
    land = [scratch[p * (levels + 1) + 1:(p + 1) * (levels + 1)] for p in range(parts)]
    sent, landed = scratch[-2], scratch[-1]
    me = lax.axis_index("dp")
    side = [(me // (1 << bit)) % 2 for bit in range(levels)]
    greet_partners(me, levels)

    def bases(p):
        base, found = 0, [0]
        for s in range(1, levels):
            base = base + side[orders[p][s]] * (1 << (levels - 1 - s))
            found.append(base)
        return found

    base_of = [bases(p) for p in range(parts)]

    def copy_of(p, s):
        bit = orders[p][s]
        if s == 0:
            source = ins[p].at[:, 1 - side[0]]
        else:
            half = 1 << (levels - 1 - s)
            source = kept[p].at[
                pl.ds(base_of[p][s - 1] + (1 - side[bit]) * half, half)
            ]
        return pltpu.make_async_remote_copy(
            src_ref=source, dst_ref=land[p][s],
            send_sem=sent.at[p, s], recv_sem=landed.at[p, s],
            device_id=(partner_of(me, bit),), device_id_type=MESH,
        )

    def add(p, s):
        total = 1 << (levels - 1 - s)
        if s == 0:

            def step(j, carry):
                chip = 0
                for i in range(1, levels):
                    chip = chip + ((j // (1 << (levels - 1 - i))) % 2) * (1 << (orders[p][i] - 1))
                kept[p][j] = (
                    ins[p][chip, side[0]].astype(jnp.float32) + land[p][0][chip].astype(jnp.float32)
                ).astype(jnp.bfloat16)
                return carry

            lax.fori_loop(0, total, step, 0)
            return
        own = base_of[p][s]
        if s < levels - 1:

            def step(j, carry):
                kept[p][own + j] = (
                    kept[p][own + j].astype(jnp.float32) + land[p][s][j].astype(jnp.float32)
                ).astype(jnp.bfloat16)
                return carry

            lax.fori_loop(0, total, step, 0)
            return
        final = kept[p][own].astype(jnp.float32) + land[p][s][0].astype(jnp.float32)
        if p < parts - 1:
            width = final.shape[1]
            qkv_out[:, p * width:(p + 1) * width] = final
        else:
            last_out[...] = final

    for s in range(levels + 1):
        for p in range(parts):
            if s > 0:
                copy_of(p, s - 1).wait_recv()
                add(p, s - 1)
            if s < levels:
                copy_of(p, s).start()
    for p in range(parts):
        for s in range(levels):
            copy_of(p, s).wait_send()


def reduce_rows(parts, devices):
    levels = devices.bit_length() - 1
    bits = list(range(1, levels))
    orders = []
    for p in range(len(parts)):
        first = bits[:3]
        turn = p % len(first)
        orders.append([0] + first[turn:] + first[:turn] + bits[3:])
    shaped = [
        part.reshape(devices // 2, 2, part.shape[0] // devices, part.shape[1]) for part in parts
    ]
    vmem = pl.BlockSpec(memory_space=pltpu.VMEM)
    scratch = []
    for part in shaped:
        scratch.append(pltpu.VMEM((devices // 2,) + part.shape[2:], jnp.bfloat16))
        for s in range(levels):
            scratch.append(pltpu.VMEM((1 << (levels - 1 - s),) + part.shape[2:], jnp.bfloat16))
    count = len(parts)
    scratch += [pltpu.SemaphoreType.DMA((count, levels))] * 2
    qkv, last = shaped[0].shape, shaped[-1].shape
    return pl.pallas_call(
        functools.partial(reduce_kernel, orders),
        out_shape=(
            jax.ShapeDtypeStruct((qkv[2], (count - 1) * qkv[3]), jnp.float32),
            jax.ShapeDtypeStruct(last[2:], jnp.float32),
        ),
        in_specs=[vmem] * count,
        out_specs=(vmem, vmem),
        scratch_shapes=scratch,
        compiler_params=pltpu.CompilerParams(
            collective_id=1, has_side_effects=True, vmem_limit_bytes=56 * 2**20
        ),
    )(*shaped)


def dot(a, b, dims=((1,), (0,))):
    return lax.dot_general(a, b, (dims, ((), ())), preferred_element_type=jnp.float32)


ROWS = ((0,), (0,))
COLS = ((1,), (1,))


def block_layout(tags, images, levels):
    position = lax.broadcasted_iota(jnp.int32, (1, BLOCK), 1).astype(jnp.float32)
    start = jnp.zeros((1, BLOCK), jnp.float32)
    segment = jnp.full((1, BLOCK), -1.0, jnp.float32)
    offset = jnp.zeros((1, BLOCK), jnp.float32)
    span = jnp.ones((1, BLOCK), jnp.float32)
    for j in range(images):
        columns = tags[2 * j + 1:2 * j + 2]
        end = start + tags[2 * j:2 * j + 1] * columns
        member = (position >= start) & (position < end)
        segment = jnp.where(member, float(j), segment)
        offset = jnp.where(member, position - start, offset)
        span = jnp.where(member, columns, span)
        start = end
    row = jnp.floor((offset + 0.5) / span)
    col = offset - row * span
    inside = segment >= 0.0
    level = lax.broadcasted_iota(jnp.int32, (2 * levels, BLOCK), 0).astype(jnp.float32)
    wanted = jnp.where(level < levels, row, col + levels)
    hot = jnp.where((level == wanted) & inside, 1.0, 0.0).astype(jnp.bfloat16)
    kind = lax.broadcasted_iota(jnp.int32, (8, BLOCK), 0).astype(jnp.float32) - 1.0
    kinds = jnp.where(kind == segment, 1.0, 0.0).astype(jnp.bfloat16)
    return hot, kinds, inside


def layer_kernel(
    images, patches_ref, tags_ref, row_ref, col_ref, gain_ref, bias_ref, w_qkv_ref, b_qkv_ref,
    w_out_ref, b_out_ref, cot_ref, out_ref, gq_ref, gk_ref, gv_ref, go_ref,
    x_s, normed_s, grad_s, qkv_s, ag_s, att_s, dqkv_s, same_s,
):
    blocks = patches_ref.shape[0]
    inner, width = w_out_ref.shape
    heads = inner // HEAD
    rows_total = blocks * BLOCK
    levels = row_ref.shape[0]
    tables = jnp.concatenate([row_ref[...], col_ref[...]], axis=0)
    scale = 1.0 / math.sqrt(HEAD)

    def embed(b, carry):
        rows = pl.ds(pl.multiple_of(b * BLOCK, BLOCK), BLOCK)
        tags = tags_ref[b]
        hot, kinds, inside = block_layout(tags, images, levels)
        live = tags[8:9]
        same_s[b] = dot(kinds, kinds, ROWS)
        wanted = jnp.where(inside, live, 0.0)
        first = lax.broadcasted_iota(jnp.int32, (8, BLOCK), 0) == 0
        wanted = jnp.where(first, wanted, 0.0).astype(jnp.bfloat16)
        keep = dot(wanted, jnp.ones((8, BLOCK), jnp.bfloat16), ROWS)[:, :1]
        grad_s[rows, :] = jnp.where(keep > 0.5, cot_ref[rows, :].astype(jnp.float32), 0.0).astype(
            jnp.bfloat16
        )
        x = (patches_ref[b].astype(jnp.float32) + dot(hot, tables, ROWS)).astype(jnp.bfloat16)
        x_s[rows, :] = x
        x = x.astype(jnp.float32)
        centred = x - jnp.mean(x, axis=-1, keepdims=True)
        variance = jnp.mean(centred * centred, axis=-1, keepdims=True)
        normed_s[rows, :] = (
            centred * lax.rsqrt(variance + EPSILON) * gain_ref[...].astype(jnp.float32)
            + bias_ref[...].astype(jnp.float32)
        ).astype(jnp.bfloat16)
        return carry

    lax.fori_loop(0, blocks, embed, 0)
    for p in range(3):
        part = slice(p * inner, (p + 1) * inner)
        qkv_s[:, part] = (
            dot(normed_s[...], w_qkv_ref[:, part]) + b_qkv_ref[:, part].astype(jnp.float32)
        ).astype(jnp.bfloat16)
    ag_s[...] = dot(grad_s[...], w_out_ref[...], COLS).astype(jnp.bfloat16)

    def attend(b, carry):
        rows = pl.ds(pl.multiple_of(b * BLOCK, BLOCK), BLOCK)
        same = same_s[b] > 0.5
        qkv = qkv_s[rows, :]
        outer = ag_s[rows, :]
        found = [[], [], [], []]
        for h in range(heads):
            part = [qkv[:, p * inner + h * HEAD:p * inner + (h + 1) * HEAD] for p in range(3)]
            query, key, value = part
            given = outer[:, h * HEAD:(h + 1) * HEAD]
            scores = jnp.where(same, dot(query, key, COLS) * scale, -1e30)
            expo = jnp.exp(scores - jnp.max(scores, axis=-1, keepdims=True))
            probs = expo / jnp.sum(expo, axis=-1, keepdims=True)
            probs_b = probs.astype(jnp.bfloat16)
            found[3].append(dot(probs_b, value).astype(jnp.bfloat16))
            prob_grad = dot(given, value, COLS)
            score_grad = (
                probs * (prob_grad - jnp.sum(prob_grad * probs, axis=-1, keepdims=True)) * scale
            ).astype(jnp.bfloat16)
            found[0].append(dot(score_grad, key).astype(jnp.bfloat16))
            found[1].append(dot(score_grad, query, ROWS).astype(jnp.bfloat16))
            found[2].append(dot(probs_b, given, ROWS).astype(jnp.bfloat16))
        for p in range(3):
            dqkv_s[rows, p * inner:(p + 1) * inner] = jnp.concatenate(found[p], axis=1)
        att_s[rows, :] = jnp.concatenate(found[3], axis=1)
        return carry

    lax.fori_loop(0, blocks, attend, 0)

    def project(b, carry):
        rows = pl.ds(pl.multiple_of(b * BLOCK, BLOCK), BLOCK)
        live = jnp.concatenate([tags_ref[b][8:9]] * (width // BLOCK), axis=1)
        projected = dot(att_s[rows, :], w_out_ref[...]) + b_out_ref[...].astype(jnp.float32)
        total = x_s[rows, :].astype(jnp.float32) + projected
        out_ref[rows, :] = jnp.where(live > 0.5, total, 0.0).astype(jnp.bfloat16)
        return carry

    lax.fori_loop(0, blocks, project, 0)
    tile = 2 * BLOCK

    def weigh(i, carry):
        rows = pl.ds(pl.multiple_of(i * tile, tile), tile)
        for p, target in enumerate((gq_ref, gk_ref, gv_ref)):
            target[rows, :] = dot(
                normed_s[:, rows], dqkv_s[:, p * inner:(p + 1) * inner], ROWS
            ).astype(jnp.bfloat16)
        return carry

    lax.fori_loop(0, width // tile, weigh, 0)

    def weigh_out(i, carry):
        rows = pl.ds(pl.multiple_of(i * BLOCK, BLOCK), BLOCK)
        go_ref[rows, :] = dot(att_s[:, rows], grad_s[...], ROWS).astype(jnp.bfloat16)
        return carry

    lax.fori_loop(0, inner // BLOCK, weigh_out, 0)


def layer(images, patches, tags, row_table, col_table, gain, bias, w_qkv, b_qkv, w_out, b_out, cot):
    rows, width = cot.shape
    inner = w_out.shape[0]
    vmem = pl.BlockSpec(memory_space=pltpu.VMEM)
    half = jnp.bfloat16
    return pl.pallas_call(
        functools.partial(layer_kernel, images),
        out_shape=(
            jax.ShapeDtypeStruct((rows, width), half),
            jax.ShapeDtypeStruct((width, inner), half),
            jax.ShapeDtypeStruct((width, inner), half),
            jax.ShapeDtypeStruct((width, inner), half),
            jax.ShapeDtypeStruct((inner, width), half),
        ),
        in_specs=[vmem] * 11,
        out_specs=(vmem,) * 5,
        scratch_shapes=[
            pltpu.VMEM((rows, width), half),
            pltpu.VMEM((rows, width), half),
            pltpu.VMEM((rows, width), half),
            pltpu.VMEM((rows, 3 * inner), half),
            pltpu.VMEM((rows, inner), half),
            pltpu.VMEM((rows, inner), half),
            pltpu.VMEM((rows, 3 * inner), half),
            pltpu.VMEM((rows // BLOCK, BLOCK, BLOCK), jnp.float32),
        ],
        compiler_params=pltpu.CompilerParams(vmem_limit_bytes=56 * 2**20),
    )(
        patches, tags, row_table, col_table, gain.reshape(1, -1), bias.reshape(1, -1),
        w_qkv, b_qkv.reshape(1, -1), w_out, b_out.reshape(1, -1), cot,
    )


def local(
    patches,
    patch_grids,
    block_counts,
    send_counts,
    row_table,
    col_table,
    ln_gain,
    ln_bias,
    w_qkv,
    b_qkv,
    w_out,
    b_out,
    cotangent,
):
    balanced = cotangent.shape[0] // BLOCK
    width = patches.shape[1]
    devices = lax.axis_size("dp")
    images = patch_grids.shape[1]
    marks = jnp.broadcast_to(
        patch_grids.reshape(-1, 2 * images, 1).astype(jnp.float32),
        (patch_grids.shape[0], 2 * images, BLOCK),
    )
    rows, tags = balance(patches, marks, block_counts, send_counts, balanced)
    result, *parts = layer(
        images, rows.reshape(balanced, BLOCK, width), tags, row_table, col_table,
        ln_gain, ln_bias, w_qkv, b_qkv, w_out, b_out, cotangent,
    )
    qkv_rows, out_rows = reduce_rows(parts, devices)
    return (result, qkv_rows, out_rows)


def solution(mesh):
    return jax.shard_map(
        local,
        mesh=mesh,
        in_specs=(
            P("dp", None),
            P("dp", None, None),
            P(),
            P(),
            P(),
            P(),
            P(),
            P(),
            P(),
            P(),
            P(),
            P(),
            P("dp", None),
        ),
        out_specs=(P("dp", None), P("dp", None), P("dp", None)),
        check_vma=False,
    )
```

```python
import functools
import math

import jax
import jax.numpy as jnp
from jax import lax
from jax.experimental import pallas as pl
from jax.experimental.pallas import tpu as pltpu
from jax.sharding import PartitionSpec as P

HEAD = 80
BLOCK = 128
CHUNKS = 8
GROUP = 8
BALANCE_MIB = 20
LAYER_MIB = 40
REDUCE_MIB = 30
EPSILON = 1e-06
MESH = pl.DeviceIdType.MESH


def partner_of(me, bit):
    own = (me // (1 << bit)) % 2
    return me + (1 - 2 * own) * (1 << bit)


def greet_partners(me, bits):
    barrier = pltpu.get_barrier_semaphore()
    for bit in range(bits):
        pl.semaphore_signal(
            barrier, inc=1, device_id=(partner_of(me, bit),), device_id_type=MESH
        )
    pl.semaphore_wait(barrier, bits)


def balance_kernel(
    sections, counts_ref, sends_ref, patches_ref, marks_ref, rows_ref, tags_ref,
    slots, slot_tags, stage, stage_tags, land, land_tags, sent, landed, sent_tags, landed_tags,
):
    me = lax.axis_index("dp")
    slot_count, chunks = patches_ref.shape[0], patches_ref.shape[1]
    balanced = rows_ref.shape[0]
    spare = stage.shape[2]
    partners = [partner_of(me, q) for q in range(sections)]
    count = counts_ref[me]
    counts, leaving = [], []
    for q in range(sections):
        counts.append(count)
        leaving.append(sends_ref[q, me])
        count = count - sends_ref[q, me] + sends_ref[q, partners[q]]
    greet_partners(me, sections)

    def copies(q, k):
        made = [
            pltpu.make_async_remote_copy(
                src_ref=stage.at[q, k], dst_ref=land.at[q, k],
                send_sem=sent.at[q, k], recv_sem=landed.at[q, k],
                device_id=(partners[q],), device_id_type=MESH,
            )
        ]
        if k == 0:
            made.append(
                pltpu.make_async_remote_copy(
                    src_ref=stage_tags.at[q], dst_ref=land_tags.at[q],
                    send_sem=sent_tags.at[q], recv_sem=landed_tags.at[q],
                    device_id=(partners[q],), device_id_type=MESH,
                )
            )
        return made

    def settle(q, k, source, arrived, target, limit):
        for s in range(limit):
            fresh = arrived[0]
            for i in range(1, spare):
                fresh = jnp.where(s - counts[q] >= i, arrived[i], fresh)
            target(s, jnp.where(s < counts[q], source(s), fresh))

    def finish(q, k):
        for copy in copies(q, k):
            copy.wait_recv()
        last = q == sections - 1
        limit = balanced if last else slot_count
        blocks = patches_ref if q == 0 else slots
        out = rows_ref if last else slots

        def put(s, value):
            out[s, k] = value

        settle(q, k, lambda s: blocks[s, k], [land[q, k, i] for i in range(spare)], put, limit)
        if k == 0:
            tags = marks_ref if q == 0 else slot_tags
            out_tags = tags_ref if last else slot_tags

            def put_tags(s, value):
                if last:
                    out_tags[s, :8] = value
                    out_tags[s, 8:] = jnp.full(value.shape, jnp.where(s < count, 1.0, 0.0))
                else:
                    out_tags[s] = value

            settle(q, k, lambda s: tags[s], [land_tags[q, i] for i in range(spare)], put_tags, limit)

    def start(q, k):
        blocks = patches_ref if q == 0 else slots
        tags = marks_ref if q == 0 else slot_tags
        for i in range(spare):
            picked = jnp.clip(counts[q] - leaving[q] + i, 0, slot_count - 1)
            stage[q, k, i] = blocks[picked, k]
            if k == 0:
                stage_tags[q, i] = tags[picked]
        for copy in copies(q, k):
            copy.start()

    for t in range(chunks + 2 * (sections - 1)):
        for q in range(sections):
            k = t - 2 * q
            if 0 <= k < chunks:
                if q > 0:
                    finish(q - 1, k)
                start(q, k)
    for k in range(chunks):
        finish(sections - 1, k)
    for q in range(sections):
        for k in range(chunks):
            for copy in copies(q, k):
                copy.wait_send()


def balance(patches, marks, block_counts, send_counts, balanced):
    slot_count = marks.shape[0]
    width = patches.shape[1]
    sections = send_counts.shape[0]
    spare = slot_count - balanced
    rows = BLOCK // CHUNKS
    vmem = pl.BlockSpec(memory_space=pltpu.VMEM)
    smem = pl.BlockSpec(memory_space=pltpu.SMEM)
    tag = marks.shape[1:]
    return pl.pallas_call(
        functools.partial(balance_kernel, sections),
        out_shape=(
            jax.ShapeDtypeStruct((balanced, CHUNKS, rows, width), patches.dtype),
            jax.ShapeDtypeStruct((balanced, 2 * tag[0], tag[1]), marks.dtype),
        ),
        in_specs=[smem, smem, vmem, vmem],
        out_specs=(vmem, vmem),
        scratch_shapes=[
            pltpu.VMEM((slot_count, CHUNKS, rows, width), patches.dtype),
            pltpu.VMEM((slot_count,) + tag, marks.dtype),
            pltpu.VMEM((sections, CHUNKS, spare, rows, width), patches.dtype),
            pltpu.VMEM((sections, spare) + tag, marks.dtype),
            pltpu.VMEM((sections, CHUNKS, spare, rows, width), patches.dtype),
            pltpu.VMEM((sections, spare) + tag, marks.dtype),
            pltpu.SemaphoreType.DMA((sections, CHUNKS)),
            pltpu.SemaphoreType.DMA((sections, CHUNKS)),
            pltpu.SemaphoreType.DMA((sections,)),
            pltpu.SemaphoreType.DMA((sections,)),
        ],
        compiler_params=pltpu.CompilerParams(
            collective_id=0, has_side_effects=True, vmem_limit_bytes=BALANCE_MIB * 2**20
        ),
    )(block_counts, send_counts, patches.reshape(slot_count, CHUNKS, rows, width), marks)


def reduce_kernel(orders, pieces, *refs):
    parts = len(orders)
    levels = len(orders[0])
    whole = pieces[-1][0] + 1
    ins, refs = refs[:whole], refs[whole:]
    qkv_out, last_out = refs[0], refs[1]
    scratch = refs[2:]
    kept = [scratch[p * (levels + 1)] for p in range(parts)]
    land = [scratch[p * (levels + 1) + 1:(p + 1) * (levels + 1)] for p in range(parts)]
    sent, landed = scratch[-2], scratch[-1]
    me = lax.axis_index("dp")
    side = [(me // (1 << bit)) % 2 for bit in range(levels)]
    greet_partners(me, levels)

    def bases(p):
        base, found = 0, [0]
        for s in range(1, levels):
            base = base + side[orders[p][s]] * (1 << (levels - 1 - s))
            found.append(base)
        return found

    base_of = [bases(p) for p in range(parts)]

    def copy_of(p, s):
        bit = orders[p][s]
        if s == 0:
            source = ins[pieces[p][0]].at[:, 1 - side[0], :, pieces[p][1]]
        else:
            half = 1 << (levels - 1 - s)
            source = kept[p].at[
                pl.ds(base_of[p][s - 1] + (1 - side[bit]) * half, half)
            ]
        return pltpu.make_async_remote_copy(
            src_ref=source, dst_ref=land[p][s],
            send_sem=sent.at[p, s], recv_sem=landed.at[p, s],
            device_id=(partner_of(me, bit),), device_id_type=MESH,
        )

    def add(p, s):
        total = 1 << (levels - 1 - s)
        if s == 0:

            def step(j, carry):
                chip = 0
                for i in range(1, levels):
                    chip = chip + ((j // (1 << (levels - 1 - i))) % 2) * (1 << (orders[p][i] - 1))
                kept[p][j] = (
                    ins[pieces[p][0]][chip, side[0], :, pieces[p][1]].astype(jnp.float32) + land[p][0][chip].astype(jnp.float32)
                ).astype(jnp.bfloat16)
                return carry

            lax.fori_loop(0, total, step, 0)
            return
        own = base_of[p][s]
        if s < levels - 1:

            def step(j, carry):
                kept[p][own + j] = (
                    kept[p][own + j].astype(jnp.float32) + land[p][s][j].astype(jnp.float32)
                ).astype(jnp.bfloat16)
                return carry

            lax.fori_loop(0, total, step, 0)
            return
        final = kept[p][own].astype(jnp.float32) + land[p][s][0].astype(jnp.float32)
        source, columns = pieces[p]
        if source < whole - 1:
            width = final.shape[1]
            qkv_out[:, source * width:(source + 1) * width] = final
        else:
            last_out[:, columns] = final

    for s in range(levels + 1):
        for p in range(parts):
            if s > 0:
                copy_of(p, s - 1).wait_recv()
                add(p, s - 1)
            if s < levels:
                copy_of(p, s).start()
    for p in range(parts):
        for s in range(levels):
            copy_of(p, s).wait_send()


def reduce_rows(parts, last, devices):
    levels = devices.bit_length() - 1
    bits = list(range(1, levels))
    shaped = [
        part.reshape(devices // 2, 2, part.shape[0] // devices, part.shape[1]) for part in parts
    ]
    shaped.append(last.reshape(devices // 2, 2, last.shape[1], last.shape[2]))
    count = len(shaped)
    pieces = [(p, slice(0, part.shape[1])) for p, part in enumerate(parts)]
    tiles = last.shape[2] // BLOCK
    ends = [tiles * i // 3 * BLOCK for i in range(4)]
    pieces += [(count - 1, slice(ends[i], ends[i + 1])) for i in range(3)]
    orders = []
    for p in range(len(pieces)):
        first = bits[:3]
        turn = p % len(first)
        orders.append([0] + first[turn:] + first[:turn] + bits[3:])
    vmem = pl.BlockSpec(memory_space=pltpu.VMEM)
    scratch = []
    for source, columns in pieces:
        tile = (shaped[source].shape[2], columns.stop - columns.start)
        scratch.append(pltpu.VMEM((devices // 2,) + tile, jnp.bfloat16))
        for s in range(levels):
            scratch.append(pltpu.VMEM((1 << (levels - 1 - s),) + tile, jnp.bfloat16))
    scratch += [pltpu.SemaphoreType.DMA((len(pieces), levels))] * 2
    qkv = shaped[0].shape
    return pl.pallas_call(
        functools.partial(reduce_kernel, orders, pieces),
        out_shape=(
            jax.ShapeDtypeStruct((qkv[2], (count - 1) * qkv[3]), jnp.float32),
            jax.ShapeDtypeStruct(last.shape[1:], jnp.float32),
        ),
        in_specs=[vmem] * count,
        out_specs=(vmem, vmem),
        scratch_shapes=scratch,
        compiler_params=pltpu.CompilerParams(
            collective_id=1, has_side_effects=True, vmem_limit_bytes=REDUCE_MIB * 2**20
        ),
    )(*shaped)


def dot(a, b, dims=((1,), (0,))):
    return lax.dot_general(a, b, (dims, ((), ())), preferred_element_type=jnp.float32)


ROWS = ((0,), (0,))
COLS = ((1,), (1,))


def block_layout(tags, images, levels):
    position = lax.broadcasted_iota(jnp.int32, (1, BLOCK), 1).astype(jnp.float32)
    start = jnp.zeros((1, BLOCK), jnp.float32)
    segment = jnp.full((1, BLOCK), -1.0, jnp.float32)
    offset = jnp.zeros((1, BLOCK), jnp.float32)
    span = jnp.ones((1, BLOCK), jnp.float32)
    for j in range(images):
        columns = tags[2 * j + 1:2 * j + 2]
        end = start + tags[2 * j:2 * j + 1] * columns
        member = (position >= start) & (position < end)
        segment = jnp.where(member, float(j), segment)
        offset = jnp.where(member, position - start, offset)
        span = jnp.where(member, columns, span)
        start = end
    row = jnp.floor((offset + 0.5) / span)
    col = offset - row * span
    inside = segment >= 0.0
    level = lax.broadcasted_iota(jnp.int32, (2 * levels, BLOCK), 0).astype(jnp.float32)
    wanted = jnp.where(level < levels, row, col + levels)
    hot = jnp.where((level == wanted) & inside, 1.0, 0.0).astype(jnp.bfloat16)
    kind = lax.broadcasted_iota(jnp.int32, (8, BLOCK), 0).astype(jnp.float32) - 1.0
    kinds = jnp.where(kind == segment, 1.0, 0.0).astype(jnp.bfloat16)
    return hot, kinds, inside


def layer_kernel(
    images, patches_ref, tags_ref, row_ref, col_ref, vector_ref, w_qkv_ref, w_out_ref, cot_ref, out_ref, gq_ref, gk_ref, gv_ref, go_ref,
    x_s, normed_s, grad_s, qkv_s, ag_s, att_s, dqkv_s, same_s,
):
    blocks = patches_ref.shape[0]
    inner, width = w_out_ref.shape
    heads = inner // HEAD
    rows_total = blocks * BLOCK
    levels = row_ref.shape[0]
    tables = jnp.concatenate([row_ref[...], col_ref[...]], axis=0)
    scale = 1.0 / math.sqrt(HEAD)
    vectors = vector_ref[...].astype(jnp.float32)
    gain, bias, b_out = (vectors[:, i * width:(i + 1) * width] for i in range(3))
    b_qkv = vectors[:, 3 * width:]

    def embed(b, carry):
        rows = pl.ds(pl.multiple_of(b * BLOCK, BLOCK), BLOCK)
        tags = tags_ref[b]
        hot, kinds, inside = block_layout(tags, images, levels)
        live = tags[8:9]
        same_s[b] = dot(kinds, kinds, ROWS)
        wanted = jnp.where(inside, live, 0.0)
        first = lax.broadcasted_iota(jnp.int32, (8, BLOCK), 0) == 0
        wanted = jnp.where(first, wanted, 0.0).astype(jnp.bfloat16)
        keep = dot(wanted, jnp.ones((8, BLOCK), jnp.bfloat16), ROWS)[:, :1]
        grad_s[rows, :] = jnp.where(keep > 0.5, cot_ref[rows, :].astype(jnp.float32), 0.0).astype(
            jnp.bfloat16
        )
        x = (patches_ref[b].astype(jnp.float32) + dot(hot, tables, ROWS)).astype(jnp.bfloat16)
        x_s[rows, :] = x
        x = x.astype(jnp.float32)
        centred = x - jnp.mean(x, axis=-1, keepdims=True)
        variance = jnp.mean(centred * centred, axis=-1, keepdims=True)
        normed_s[rows, :] = (
            centred * lax.rsqrt(variance + EPSILON) * gain
            + bias
        ).astype(jnp.bfloat16)
        return carry

    lax.fori_loop(0, blocks, embed, 0)
    for p in range(3):
        part = slice(p * inner, (p + 1) * inner)
        qkv_s[:, part] = (
            dot(normed_s[...], w_qkv_ref[:, part]) + b_qkv[:, part]
        ).astype(jnp.bfloat16)
    ag_s[...] = dot(grad_s[...], w_out_ref[...], COLS).astype(jnp.bfloat16)

    def attend(b, carry):
        rows = pl.ds(pl.multiple_of(b * BLOCK, BLOCK), BLOCK)
        same = same_s[b] > 0.5
        qkv = qkv_s[rows, :]
        outer = ag_s[rows, :]
        found = [[], [], [], []]
        for first in range(0, heads, GROUP):
            group = range(first, first + GROUP)
            query, key, value = (
                [qkv[:, p * inner + h * HEAD:p * inner + (h + 1) * HEAD] for h in group]
                for p in range(3)
            )
            given = [outer[:, h * HEAD:(h + 1) * HEAD] for h in group]
            scores = [dot(q, k, COLS) for q, k in zip(query, key)]
            prob_grad = [dot(g, v, COLS) for g, v in zip(given, value)]
            scores = [jnp.where(same, s * scale, -1e30) for s in scores]
            expo = [jnp.exp(s - jnp.max(s, axis=-1, keepdims=True)) for s in scores]
            probs = [e * (1.0 / jnp.sum(e, axis=-1, keepdims=True)) for e in expo]
            probs_b = [p.astype(jnp.bfloat16) for p in probs]
            score_grad = [
                (p * (g - jnp.sum(g * p, axis=-1, keepdims=True)) * scale).astype(jnp.bfloat16)
                for p, g in zip(probs, prob_grad)
            ]
            found[3] += [dot(p, v).astype(jnp.bfloat16) for p, v in zip(probs_b, value)]
            found[2] += [dot(p, g, ROWS).astype(jnp.bfloat16) for p, g in zip(probs_b, given)]
            found[0] += [dot(s, k).astype(jnp.bfloat16) for s, k in zip(score_grad, key)]
            found[1] += [dot(s, q, ROWS).astype(jnp.bfloat16) for s, q in zip(score_grad, query)]
        for p in range(3):
            dqkv_s[rows, p * inner:(p + 1) * inner] = jnp.concatenate(found[p], axis=1)
        att_s[rows, :] = jnp.concatenate(found[3], axis=1)
        return carry

    lax.fori_loop(0, blocks, attend, 0)

    def project(b, carry):
        rows = pl.ds(pl.multiple_of(b * BLOCK, BLOCK), BLOCK)
        live = jnp.concatenate([tags_ref[b][8:9]] * (width // BLOCK), axis=1)
        projected = dot(att_s[rows, :], w_out_ref[...]) + b_out
        total = x_s[rows, :].astype(jnp.float32) + projected
        out_ref[rows, :] = jnp.where(live > 0.5, total, 0.0).astype(jnp.bfloat16)
        return carry

    lax.fori_loop(0, blocks, project, 0)
    tile = 2 * BLOCK

    def weigh(i, carry):
        rows = pl.ds(pl.multiple_of(i * tile, tile), tile)
        for p, target in enumerate((gq_ref, gk_ref, gv_ref)):
            target[rows, :] = dot(
                normed_s[:, rows], dqkv_s[:, p * inner:(p + 1) * inner], ROWS
            ).astype(jnp.bfloat16)
        return carry

    lax.fori_loop(0, width // tile, weigh, 0)

    ranks, share = go_ref.shape[0], go_ref.shape[1]

    for first in range(0, width, inner):
        total = dot(att_s[...], grad_s[:, first:first + inner], ROWS)
        for r in range(ranks):
            go_ref[r, :, first:first + inner] = total[r * share:(r + 1) * share].astype(
                jnp.bfloat16
            )


def layer(images, devices, patches, tags, row_table, col_table, gain, bias, w_qkv, b_qkv, w_out, b_out, cot):
    rows, width = cot.shape
    inner = w_out.shape[0]
    vmem = pl.BlockSpec(memory_space=pltpu.VMEM)
    half = jnp.bfloat16
    return pl.pallas_call(
        functools.partial(layer_kernel, images),
        out_shape=(
            jax.ShapeDtypeStruct((rows, width), half),
            jax.ShapeDtypeStruct((width, inner), half),
            jax.ShapeDtypeStruct((width, inner), half),
            jax.ShapeDtypeStruct((width, inner), half),
            jax.ShapeDtypeStruct((devices, inner // devices, width), half),
        ),
        in_specs=[vmem] * 8,
        out_specs=(vmem,) * 5,
        scratch_shapes=[
            pltpu.VMEM((rows, width), half),
            pltpu.VMEM((rows, width), half),
            pltpu.VMEM((rows, width), half),
            pltpu.VMEM((rows, 3 * inner), half),
            pltpu.VMEM((rows, inner), half),
            pltpu.VMEM((rows, inner), half),
            pltpu.VMEM((rows, 3 * inner), half),
            pltpu.VMEM((rows // BLOCK, BLOCK, BLOCK), jnp.float32),
        ],
        compiler_params=pltpu.CompilerParams(vmem_limit_bytes=LAYER_MIB * 2**20),
    )(
        patches, tags, row_table, col_table,
        jnp.concatenate([gain, bias, b_out, b_qkv]).reshape(1, -1), w_qkv, w_out, cot,
    )


def local(
    patches,
    patch_grids,
    block_counts,
    send_counts,
    row_table,
    col_table,
    ln_gain,
    ln_bias,
    w_qkv,
    b_qkv,
    w_out,
    b_out,
    cotangent,
):
    balanced = cotangent.shape[0] // BLOCK
    width = patches.shape[1]
    devices = lax.axis_size("dp")
    images = patch_grids.shape[1]
    marks = jnp.broadcast_to(
        patch_grids.reshape(-1, 2 * images, 1).astype(jnp.float32),
        (patch_grids.shape[0], 2 * images, BLOCK),
    )
    rows, tags = balance(patches, marks, block_counts, send_counts, balanced)
    result, *parts = layer(
        images, devices, rows.reshape(balanced, BLOCK, width), tags, row_table, col_table,
        ln_gain, ln_bias, w_qkv, b_qkv, w_out, b_out, cotangent,
    )
    qkv_rows, out_rows = reduce_rows(parts[:-1], parts[-1], devices)
    return (result, qkv_rows, out_rows)


def solution(mesh):
    return jax.shard_map(
        local,
        mesh=mesh,
        in_specs=(
            P("dp", None),
            P("dp", None, None),
            P(),
            P(),
            P(),
            P(),
            P(),
            P(),
            P(),
            P(),
            P(),
            P(),
            P("dp", None),
        ),
        out_specs=(P("dp", None), P("dp", None), P("dp", None)),
        check_vma=False,
    )
```

```python
import functools
import math

import jax
import jax.numpy as jnp
from jax import lax
from jax.experimental import pallas as pl
from jax.experimental.pallas import tpu as pltpu
from jax.sharding import PartitionSpec as P

HEAD = 80
BLOCK = 128
CHUNKS = 8
GROUP = 8
BALANCE_MIB = 20
LAYER_MIB = 40
REDUCE_MIB = 30
EPSILON = 1e-06
MESH = pl.DeviceIdType.MESH


def partner_of(me, bit):
    own = (me // (1 << bit)) % 2
    return me + (1 - 2 * own) * (1 << bit)


def greet_partners(me, bits):
    barrier = pltpu.get_barrier_semaphore()
    for bit in range(bits):
        pl.semaphore_signal(
            barrier, inc=1, device_id=(partner_of(me, bit),), device_id_type=MESH
        )
    pl.semaphore_wait(barrier, bits)


def balance_kernel(
    sections, counts_ref, sends_ref, patches_ref, marks_ref, rows_ref, tags_ref,
    slots, slot_tags, stage, stage_tags, land, land_tags, sent, landed, sent_tags, landed_tags,
):
    me = lax.axis_index("dp")
    slot_count, chunks = patches_ref.shape[0], patches_ref.shape[1]
    balanced = rows_ref.shape[0]
    spare = stage.shape[2]
    partners = [partner_of(me, q) for q in range(sections)]
    count = counts_ref[me]
    counts, leaving = [], []
    for q in range(sections):
        counts.append(count)
        leaving.append(sends_ref[q, me])
        count = count - sends_ref[q, me] + sends_ref[q, partners[q]]
    greet_partners(me, sections)

    def copies(q, k):
        made = [
            pltpu.make_async_remote_copy(
                src_ref=stage.at[q, k], dst_ref=land.at[q, k],
                send_sem=sent.at[q, k], recv_sem=landed.at[q, k],
                device_id=(partners[q],), device_id_type=MESH,
            )
        ]
        if k == 0:
            made.append(
                pltpu.make_async_remote_copy(
                    src_ref=stage_tags.at[q], dst_ref=land_tags.at[q],
                    send_sem=sent_tags.at[q], recv_sem=landed_tags.at[q],
                    device_id=(partners[q],), device_id_type=MESH,
                )
            )
        return made

    def settle(q, k, source, arrived, target, limit):
        for s in range(limit):
            fresh = arrived[0]
            for i in range(1, spare):
                fresh = jnp.where(s - counts[q] >= i, arrived[i], fresh)
            target(s, jnp.where(s < counts[q], source(s), fresh))

    def finish(q, k):
        for copy in copies(q, k):
            copy.wait_recv()
        last = q == sections - 1
        limit = balanced if last else slot_count
        blocks = patches_ref if q == 0 else slots
        out = rows_ref if last else slots

        def put(s, value):
            out[s, k] = value

        settle(q, k, lambda s: blocks[s, k], [land[q, k, i] for i in range(spare)], put, limit)
        if k == 0:
            tags = marks_ref if q == 0 else slot_tags
            out_tags = tags_ref if last else slot_tags

            def put_tags(s, value):
                if last:
                    out_tags[s, :8] = value
                    out_tags[s, 8:] = jnp.full(value.shape, jnp.where(s < count, 1.0, 0.0))
                else:
                    out_tags[s] = value

            settle(q, k, lambda s: tags[s], [land_tags[q, i] for i in range(spare)], put_tags, limit)

    def start(q, k):
        blocks = patches_ref if q == 0 else slots
        tags = marks_ref if q == 0 else slot_tags
        for i in range(spare):
            picked = jnp.clip(counts[q] - leaving[q] + i, 0, slot_count - 1)
            stage[q, k, i] = blocks[picked, k]
            if k == 0:
                stage_tags[q, i] = tags[picked]
        for copy in copies(q, k):
            copy.start()

    for t in range(chunks + 2 * (sections - 1)):
        for q in range(sections):
            k = t - 2 * q
            if 0 <= k < chunks:
                if q > 0:
                    finish(q - 1, k)
                start(q, k)
    for k in range(chunks):
        finish(sections - 1, k)
    for q in range(sections):
        for k in range(chunks):
            for copy in copies(q, k):
                copy.wait_send()


def balance(patches, marks, block_counts, send_counts, balanced):
    slot_count = marks.shape[0]
    width = patches.shape[1]
    sections = send_counts.shape[0]
    spare = slot_count - balanced
    rows = BLOCK // CHUNKS
    vmem = pl.BlockSpec(memory_space=pltpu.VMEM)
    smem = pl.BlockSpec(memory_space=pltpu.SMEM)
    tag = marks.shape[1:]
    return pl.pallas_call(
        functools.partial(balance_kernel, sections),
        out_shape=(
            jax.ShapeDtypeStruct((balanced, CHUNKS, rows, width), patches.dtype),
            jax.ShapeDtypeStruct((balanced, 2 * tag[0], tag[1]), marks.dtype),
        ),
        in_specs=[smem, smem, vmem, vmem],
        out_specs=(vmem, vmem),
        scratch_shapes=[
            pltpu.VMEM((slot_count, CHUNKS, rows, width), patches.dtype),
            pltpu.VMEM((slot_count,) + tag, marks.dtype),
            pltpu.VMEM((sections, CHUNKS, spare, rows, width), patches.dtype),
            pltpu.VMEM((sections, spare) + tag, marks.dtype),
            pltpu.VMEM((sections, CHUNKS, spare, rows, width), patches.dtype),
            pltpu.VMEM((sections, spare) + tag, marks.dtype),
            pltpu.SemaphoreType.DMA((sections, CHUNKS)),
            pltpu.SemaphoreType.DMA((sections, CHUNKS)),
            pltpu.SemaphoreType.DMA((sections,)),
            pltpu.SemaphoreType.DMA((sections,)),
        ],
        compiler_params=pltpu.CompilerParams(
            collective_id=0, has_side_effects=True, vmem_limit_bytes=BALANCE_MIB * 2**20
        ),
    )(block_counts, send_counts, patches.reshape(slot_count, CHUNKS, rows, width), marks)


def reduce_kernel(orders, pieces, *refs):
    parts = len(orders)
    levels = len(orders[0])
    whole = max(source for source, _ in pieces) + 1
    ins, refs = refs[:whole], refs[whole:]
    qkv_out, last_out = refs[0], refs[1]
    scratch = refs[2:]
    kept = [scratch[p * (levels + 1)] for p in range(parts)]
    land = [scratch[p * (levels + 1) + 1:(p + 1) * (levels + 1)] for p in range(parts)]
    sent, landed = scratch[-2], scratch[-1]
    me = lax.axis_index("dp")
    side = [(me // (1 << bit)) % 2 for bit in range(levels)]
    greet_partners(me, levels)

    def bases(p):
        base, found = 0, [0]
        for s in range(1, levels):
            base = base + side[orders[p][s]] * (1 << (levels - 1 - s))
            found.append(base)
        return found

    base_of = [bases(p) for p in range(parts)]

    def copy_of(p, s):
        bit = orders[p][s]
        if s == 0:
            source = ins[pieces[p][0]].at[:, 1 - side[0], :, pieces[p][1]]
        else:
            half = 1 << (levels - 1 - s)
            source = kept[p].at[
                pl.ds(base_of[p][s - 1] + (1 - side[bit]) * half, half)
            ]
        return pltpu.make_async_remote_copy(
            src_ref=source, dst_ref=land[p][s],
            send_sem=sent.at[p, s], recv_sem=landed.at[p, s],
            device_id=(partner_of(me, bit),), device_id_type=MESH,
        )

    def add(p, s):
        total = 1 << (levels - 1 - s)
        if s == 0:

            def step(j, carry):
                chip = 0
                for i in range(1, levels):
                    chip = chip + ((j // (1 << (levels - 1 - i))) % 2) * (1 << (orders[p][i] - 1))
                kept[p][j] = (
                    ins[pieces[p][0]][chip, side[0], :, pieces[p][1]].astype(jnp.float32) + land[p][0][chip].astype(jnp.float32)
                ).astype(jnp.bfloat16)
                return carry

            lax.fori_loop(0, total, step, 0)
            return
        own = base_of[p][s]
        if s < levels - 1:

            def step(j, carry):
                kept[p][own + j] = (
                    kept[p][own + j].astype(jnp.float32) + land[p][s][j].astype(jnp.float32)
                ).astype(jnp.bfloat16)
                return carry

            lax.fori_loop(0, total, step, 0)
            return
        final = kept[p][own].astype(jnp.float32) + land[p][s][0].astype(jnp.float32)
        source, columns = pieces[p]
        if source < whole - 1:
            width = final.shape[1]
            qkv_out[:, source * width:(source + 1) * width] = final
        else:
            last_out[:, columns] = final

    for s in range(levels + 1):
        for p in range(parts):
            if s > 0:
                copy_of(p, s - 1).wait_recv()
                add(p, s - 1)
            if s < levels:
                copy_of(p, s).start()
    for p in range(parts):
        for s in range(levels):
            copy_of(p, s).wait_send()


def reduce_rows(parts, last, devices):
    levels = devices.bit_length() - 1
    bits = list(range(1, levels))
    shaped = [
        part.reshape(devices // 2, 2, part.shape[0] // devices, part.shape[1]) for part in parts
    ]
    shaped.append(last.reshape(devices // 2, 2, last.shape[1], last.shape[2]))
    count = len(shaped)
    pieces = [(p, slice(0, part.shape[1])) for p, part in enumerate(parts)]
    tiles = last.shape[2] // BLOCK
    ends = [tiles * i // 3 * BLOCK for i in range(4)]
    pieces += [(count - 1, slice(ends[i], ends[i + 1])) for i in range(3)]
    pieces = pieces[3:] + pieces[:3]
    orders = []
    for p in range(len(pieces)):
        first = bits[:3]
        turn = p % len(first)
        orders.append([0] + first[turn:] + first[:turn] + bits[3:])
    vmem = pl.BlockSpec(memory_space=pltpu.VMEM)
    scratch = []
    for source, columns in pieces:
        tile = (shaped[source].shape[2], columns.stop - columns.start)
        scratch.append(pltpu.VMEM((devices // 2,) + tile, jnp.bfloat16))
        for s in range(levels):
            scratch.append(pltpu.VMEM((1 << (levels - 1 - s),) + tile, jnp.bfloat16))
    scratch += [pltpu.SemaphoreType.DMA((len(pieces), levels))] * 2
    qkv = shaped[0].shape
    return pl.pallas_call(
        functools.partial(reduce_kernel, orders, pieces),
        out_shape=(
            jax.ShapeDtypeStruct((qkv[2], (count - 1) * qkv[3]), jnp.float32),
            jax.ShapeDtypeStruct(last.shape[1:], jnp.float32),
        ),
        in_specs=[vmem] * count,
        out_specs=(vmem, vmem),
        scratch_shapes=scratch,
        compiler_params=pltpu.CompilerParams(
            collective_id=1, has_side_effects=True, vmem_limit_bytes=REDUCE_MIB * 2**20
        ),
    )(*shaped)


def dot(a, b, dims=((1,), (0,))):
    return lax.dot_general(a, b, (dims, ((), ())), preferred_element_type=jnp.float32)


ROWS = ((0,), (0,))
COLS = ((1,), (1,))


def block_layout(tags, images, levels):
    position = lax.broadcasted_iota(jnp.int32, (1, BLOCK), 1).astype(jnp.float32)
    start = jnp.zeros((1, BLOCK), jnp.float32)
    segment = jnp.full((1, BLOCK), -1.0, jnp.float32)
    offset = jnp.zeros((1, BLOCK), jnp.float32)
    span = jnp.ones((1, BLOCK), jnp.float32)
    for j in range(images):
        columns = tags[2 * j + 1:2 * j + 2]
        end = start + tags[2 * j:2 * j + 1] * columns
        member = (position >= start) & (position < end)
        segment = jnp.where(member, float(j), segment)
        offset = jnp.where(member, position - start, offset)
        span = jnp.where(member, columns, span)
        start = end
    row = jnp.floor((offset + 0.5) / span)
    col = offset - row * span
    inside = segment >= 0.0
    level = lax.broadcasted_iota(jnp.int32, (2 * levels, BLOCK), 0).astype(jnp.float32)
    wanted = jnp.where(level < levels, row, col + levels)
    hot = jnp.where((level == wanted) & inside, 1.0, 0.0).astype(jnp.bfloat16)
    kind = lax.broadcasted_iota(jnp.int32, (8, BLOCK), 0).astype(jnp.float32) - 1.0
    kinds = jnp.where(kind == segment, 1.0, 0.0).astype(jnp.bfloat16)
    return hot, kinds, inside


def layer_kernel(
    images, patches_ref, tags_ref, row_ref, col_ref, vector_ref, w_qkv_ref, w_out_ref, cot_ref, out_ref, gq_ref, gk_ref, gv_ref, go_ref,
    x_s, normed_s, grad_s, qkv_s, ag_s, att_s, dqkv_s, same_s,
):
    blocks = patches_ref.shape[0]
    inner, width = w_out_ref.shape
    heads = inner // HEAD
    rows_total = blocks * BLOCK
    levels = row_ref.shape[0]
    tables = jnp.concatenate([row_ref[...], col_ref[...]], axis=0)
    scale = 1.0 / math.sqrt(HEAD)
    vectors = vector_ref[...].astype(jnp.float32)
    gain, bias, b_out = (vectors[:, i * width:(i + 1) * width] for i in range(3))
    b_qkv = vectors[:, 3 * width:]

    def embed(b, carry):
        rows = pl.ds(pl.multiple_of(b * BLOCK, BLOCK), BLOCK)
        tags = tags_ref[b]
        hot, kinds, inside = block_layout(tags, images, levels)
        live = tags[8:9]
        same_s[b] = dot(kinds, kinds, ROWS)
        wanted = jnp.where(inside, live, 0.0)
        first = lax.broadcasted_iota(jnp.int32, (8, BLOCK), 0) == 0
        wanted = jnp.where(first, wanted, 0.0).astype(jnp.bfloat16)
        keep = dot(wanted, jnp.ones((8, BLOCK), jnp.bfloat16), ROWS)[:, :1]
        grad_s[rows, :] = jnp.where(keep > 0.5, cot_ref[rows, :].astype(jnp.float32), 0.0).astype(
            jnp.bfloat16
        )
        x = (patches_ref[b].astype(jnp.float32) + dot(hot, tables, ROWS)).astype(jnp.bfloat16)
        x_s[rows, :] = x
        x = x.astype(jnp.float32)
        centred = x - jnp.mean(x, axis=-1, keepdims=True)
        variance = jnp.mean(centred * centred, axis=-1, keepdims=True)
        normed_s[rows, :] = (
            centred * lax.rsqrt(variance + EPSILON) * gain
            + bias
        ).astype(jnp.bfloat16)
        return carry

    lax.fori_loop(0, blocks, embed, 0)
    for p in range(3):
        part = slice(p * inner, (p + 1) * inner)
        qkv_s[:, part] = (
            dot(normed_s[...], w_qkv_ref[:, part]) + b_qkv[:, part]
        ).astype(jnp.bfloat16)
    ag_s[...] = dot(grad_s[...], w_out_ref[...], COLS).astype(jnp.bfloat16)

    def attend(b, carry):
        rows = pl.ds(pl.multiple_of(b * BLOCK, BLOCK), BLOCK)
        same = same_s[b] > 0.5
        qkv = qkv_s[rows, :]
        outer = ag_s[rows, :]
        found = [[], [], [], []]
        for first in range(0, heads, GROUP):
            group = range(first, first + GROUP)
            query, key, value = (
                [qkv[:, p * inner + h * HEAD:p * inner + (h + 1) * HEAD] for h in group]
                for p in range(3)
            )
            given = [outer[:, h * HEAD:(h + 1) * HEAD] for h in group]
            scores = [dot(q, k, COLS) for q, k in zip(query, key)]
            prob_grad = [dot(g, v, COLS) for g, v in zip(given, value)]
            scores = [jnp.where(same, s * scale, -1e30) for s in scores]
            expo = [jnp.exp(s - jnp.max(s, axis=-1, keepdims=True)) for s in scores]
            probs = [e * (1.0 / jnp.sum(e, axis=-1, keepdims=True)) for e in expo]
            probs_b = [p.astype(jnp.bfloat16) for p in probs]
            score_grad = [
                (p * (g - jnp.sum(g * p, axis=-1, keepdims=True)) * scale).astype(jnp.bfloat16)
                for p, g in zip(probs, prob_grad)
            ]
            found[3] += [dot(p, v).astype(jnp.bfloat16) for p, v in zip(probs_b, value)]
            found[2] += [dot(p, g, ROWS).astype(jnp.bfloat16) for p, g in zip(probs_b, given)]
            found[0] += [dot(s, k).astype(jnp.bfloat16) for s, k in zip(score_grad, key)]
            found[1] += [dot(s, q, ROWS).astype(jnp.bfloat16) for s, q in zip(score_grad, query)]
        for p in range(3):
            dqkv_s[rows, p * inner:(p + 1) * inner] = jnp.concatenate(found[p], axis=1)
        att_s[rows, :] = jnp.concatenate(found[3], axis=1)
        return carry

    lax.fori_loop(0, blocks, attend, 0)

    def project(b, carry):
        rows = pl.ds(pl.multiple_of(b * BLOCK, BLOCK), BLOCK)
        live = jnp.concatenate([tags_ref[b][8:9]] * (width // BLOCK), axis=1)
        projected = dot(att_s[rows, :], w_out_ref[...]) + b_out
        total = x_s[rows, :].astype(jnp.float32) + projected
        out_ref[rows, :] = jnp.where(live > 0.5, total, 0.0).astype(jnp.bfloat16)
        return carry

    lax.fori_loop(0, blocks, project, 0)
    tile = 2 * BLOCK

    def weigh(i, carry):
        rows = pl.ds(pl.multiple_of(i * tile, tile), tile)
        for p, target in enumerate((gq_ref, gk_ref, gv_ref)):
            target[rows, :] = dot(
                normed_s[:, rows], dqkv_s[:, p * inner:(p + 1) * inner], ROWS
            ).astype(jnp.bfloat16)
        return carry

    lax.fori_loop(0, width // tile, weigh, 0)

    ranks, share = go_ref.shape[0], go_ref.shape[1]

    for first in range(0, width, inner):
        total = dot(att_s[...], grad_s[:, first:first + inner], ROWS)
        for r in range(ranks):
            go_ref[r, :, first:first + inner] = total[r * share:(r + 1) * share].astype(
                jnp.bfloat16
            )


def layer(images, devices, patches, tags, row_table, col_table, gain, bias, w_qkv, b_qkv, w_out, b_out, cot):
    rows, width = cot.shape
    inner = w_out.shape[0]
    vmem = pl.BlockSpec(memory_space=pltpu.VMEM)
    half = jnp.bfloat16
    return pl.pallas_call(
        functools.partial(layer_kernel, images),
        out_shape=(
            jax.ShapeDtypeStruct((rows, width), half),
            jax.ShapeDtypeStruct((width, inner), half),
            jax.ShapeDtypeStruct((width, inner), half),
            jax.ShapeDtypeStruct((width, inner), half),
            jax.ShapeDtypeStruct((devices, inner // devices, width), half),
        ),
        in_specs=[vmem] * 8,
        out_specs=(vmem,) * 5,
        scratch_shapes=[
            pltpu.VMEM((rows, width), half),
            pltpu.VMEM((rows, width), half),
            pltpu.VMEM((rows, width), half),
            pltpu.VMEM((rows, 3 * inner), half),
            pltpu.VMEM((rows, inner), half),
            pltpu.VMEM((rows, inner), half),
            pltpu.VMEM((rows, 3 * inner), half),
            pltpu.VMEM((rows // BLOCK, BLOCK, BLOCK), jnp.float32),
        ],
        compiler_params=pltpu.CompilerParams(vmem_limit_bytes=LAYER_MIB * 2**20),
    )(
        patches, tags, row_table, col_table,
        jnp.concatenate([gain, bias, b_out, b_qkv]).reshape(1, -1), w_qkv, w_out, cot,
    )


def local(
    patches,
    patch_grids,
    block_counts,
    send_counts,
    row_table,
    col_table,
    ln_gain,
    ln_bias,
    w_qkv,
    b_qkv,
    w_out,
    b_out,
    cotangent,
):
    balanced = cotangent.shape[0] // BLOCK
    width = patches.shape[1]
    devices = lax.axis_size("dp")
    images = patch_grids.shape[1]
    marks = jnp.broadcast_to(
        patch_grids.reshape(-1, 2 * images, 1).astype(jnp.float32),
        (patch_grids.shape[0], 2 * images, BLOCK),
    )
    rows, tags = balance(patches, marks, block_counts, send_counts, balanced)
    result, *parts = layer(
        images, devices, rows.reshape(balanced, BLOCK, width), tags, row_table, col_table,
        ln_gain, ln_bias, w_qkv, b_qkv, w_out, b_out, cotangent,
    )
    qkv_rows, out_rows = reduce_rows(parts[:-1], parts[-1], devices)
    return (result, qkv_rows, out_rows)


def solution(mesh):
    return jax.shard_map(
        local,
        mesh=mesh,
        in_specs=(
            P("dp", None),
            P("dp", None, None),
            P(),
            P(),
            P(),
            P(),
            P(),
            P(),
            P(),
            P(),
            P(),
            P(),
            P("dp", None),
        ),
        out_specs=(P("dp", None), P("dp", None), P("dp", None)),
        check_vma=False,
    )
```
